128 devices in a mesh: row: 16 (over z, x), col: 8 (over y, core).
Axes of the slice: x: 4, y: 4, z: 4, core: 2. Of those that a mesh axis runs over, the one named last changes fastest.
Arguments:
- inputs: bfloat16 [1536, 28672], P('col', 'row'), may hold values from -100 to 100
- out_grads: bfloat16 [1536, 8192], P('row', 'col'), may hold values from -30 to 30
- user_ids: int32 [4], replicated, may hold values from 0 to 1, as said below
Outputs:
- orthogonalized: bfloat16 [28672, 8192], P('row', 'col')
The draws below stay inside these ranges and needn't reach their ends.
Inputs may be any that keep to these rules, and one draw needn't show every extreme that they name: `user_ids`: entry m is the user of microbatch m (rows m * 384 to (m + 1) * 384 - 1); each of the users 0 and 1 has exactly 2 microbatches.
All inputs are finite; a program needn't handle non-finite values.
Results may differ from the reference program's by a relative error of at most 0.0067.
Values may be sent and summed in bfloat16 or wider, within the bound.
A program may use at most 192 MiB of HBM per device.

```python
import math
import jax
import jax.numpy as jnp
from jax import lax

FF = 28672
D = 8192
BLOCK = 1024
MICRO = 4
MB_ROWS = 384
NS_STEPS = 2
TOKENS = 1536


def draw_inputs(key, part):
    entry_key, jitter_key, batch_key, token_key = jax.random.split(jax.random.fold_in(key, 11), 4)
    column = jnp.arange(FF, dtype=jnp.float32)
    ramp = jnp.exp(column / (FF - 1) * math.log(3.0))
    noise = jnp.clip(jax.random.normal(entry_key, (TOKENS + 1, FF), jnp.float32), -4.0, 4.0)
    jitter = jnp.exp(jax.random.uniform(jitter_key, (FF,), jnp.float32, 0.0, math.log(4.0)))
    mixed = (noise[1:] + noise[:-1]) * math.sqrt(0.5)
    batch_scale = jnp.exp(jax.random.uniform(batch_key, (MICRO,), jnp.float32, -0.6, 0.6))
    token_scale = jnp.exp(jax.random.uniform(token_key, (TOKENS,), jnp.float32, -0.25, 0.25))
    row_scale = jnp.repeat(batch_scale, MB_ROWS) * token_scale
    values = mixed * row_scale[:, None] * (ramp * jitter)[None, :]
    return jnp.clip(values, -100.0, 100.0).astype(jnp.bfloat16)


def draw_out_grads(key, part):
    entry_key, column_key = jax.random.split(jax.random.fold_in(key, 37))
    noise = jnp.clip(jax.random.normal(entry_key, (TOKENS + 1, D), jnp.float32), -4.0, 4.0)
    columns = jnp.exp(jax.random.uniform(column_key, (D,), jnp.float32, 0.0, math.log(2.0)))
    mixed = (noise[1:] + noise[:-1]) * math.sqrt(0.5)
    return (mixed * columns[None, :]).astype(jnp.bfloat16)


def draw_user_ids(key, part):
    order_key = jax.random.fold_in(key, 23)
    order = jax.random.permutation(order_key, MICRO)
    return (order < MICRO // 2).astype(jnp.int32)


def setup_inputs(seed: int = 0) -> dict:
    streams_of = jax.random.split(jax.random.key(seed), 4)
    inputs = draw_inputs(jax.random.fold_in(streams_of[3], 71), 0)
    out_grads = draw_out_grads(jax.random.fold_in(streams_of[3], 71), 0)
    user_ids = draw_user_ids(jax.random.fold_in(streams_of[3], 71), 0)
    return {"inputs": inputs, "out_grads": out_grads, "user_ids": user_ids}


target_coef = 0.15

def newton(block):
    iterate = block
    for iteration in range(NS_STEPS):
        gram_matrix = jnp.dot(iterate, iterate.T, preferred_element_type=jnp.float32).astype(jnp.bfloat16)
        product = jnp.dot(gram_matrix, iterate, preferred_element_type=jnp.float32)
        updated = 1.5 * iterate.astype(jnp.float32) - 0.5 * product
        if iteration == NS_STEPS - 1:
            updated = updated * math.sqrt(BLOCK)
        iterate = updated.astype(jnp.bfloat16)
    return iterate

def reference(inputs, out_grads, user_ids):
    grad_zero = jnp.zeros((FF, D), jnp.float32)
    grad_one = jnp.zeros((FF, D), jnp.float32)
    for batch in range(MICRO):
        rows_in = inputs[batch * MB_ROWS:(batch + 1) * MB_ROWS]
        rows_out = out_grads[batch * MB_ROWS:(batch + 1) * MB_ROWS]
        product = jnp.dot(rows_in.T, rows_out, preferred_element_type=jnp.float32)
        weight = (user_ids[batch] == 1).astype(jnp.float32)
        grad_one = grad_one + weight * product
        grad_zero = grad_zero + (1.0 - weight) * product
    grad_zero = grad_zero.astype(jnp.bfloat16)
    grad_one = grad_one.astype(jnp.bfloat16)
    squares_zero = jnp.sum(jnp.square(grad_zero.astype(jnp.float32)))
    squares_one = jnp.sum(jnp.square(grad_one.astype(jnp.float32)))
    target = target_coef * math.sqrt(FF * D / BLOCK)
    factor_zero = target / jnp.sqrt(squares_zero + 1e-06)
    factor_one = target / jnp.sqrt(squares_one + 1e-06)
    update = (factor_zero * grad_zero.astype(jnp.float32) + factor_one * grad_one.astype(jnp.float32)).astype(jnp.bfloat16)
    blocks = update.reshape(FF // BLOCK, BLOCK, D // BLOCK, BLOCK).transpose(0, 2, 1, 3).reshape(-1, BLOCK, BLOCK)
    finished = lax.map(newton, blocks)
    return finished.reshape(FF // BLOCK, D // BLOCK, BLOCK, BLOCK).transpose(0, 2, 1, 3).reshape(FF, D)
```

```python
import math

import jax
import jax.numpy as jnp
from jax import lax
from jax.experimental import pallas as pl
from jax.experimental.pallas import tpu as pltpu
from jax.sharding import Mesh
from jax.sharding import PartitionSpec as P

FF = 28672
D = 8192
BLOCK = 1024
TARGET = 0.15 * math.sqrt(FF * D / BLOCK)
LAST_SCALE = math.sqrt(BLOCK)

MESH = pl.DeviceIdType.MESH
CH = 256
OWN = 7
SLAB = 192
MB = 384
GS = 96
HALF = 512
MINUS, PLUS = 0, 1


def dot_tn(a, b):
    return lax.dot_general(a, b, (((0,), (0,)), ((), ())), preferred_element_type=jnp.float32)


def dot_nt(a, b):
    return lax.dot_general(a, b, (((1,), (1,)), ((), ())), preferred_element_type=jnp.float32)


def dot_nn(a, b):
    return lax.dot_general(a, b, (((1,), (0,)), ((), ())), preferred_element_type=jnp.float32)


def kernel(
    uids, inp, og, out,
    IN, OG, ACC, G, X, X1, A, OUTB, SQ, S1, R1, S2, R2,
    sy, ry, sf, rf, sb, rb, lc, sx, rx,
    oa1s, oa1r, of1s, of1r, oa2s, oa2r, of2s, of2r, ol,
    a1s, a1r, a2s, a2r, ret_s, ret_r, od,
):
    z, x, y, c = (lax.axis_index(a) for a in ("z", "x", "y", "c"))
    zm, zp, zf = (lax.rem(z + d, 4) for d in (3, 1, 2))
    xm, xp, xf = (lax.rem(x + d, 4) for d in (3, 1, 2))
    ym, yp, yf = (lax.rem(y + d, 4) for d in (3, 1, 2))
    sib = 1 - c
    inner = jnp.logical_or(x == 1, x == 2)
    nch = jnp.where(inner, OWN + 2, OWN + 1)
    col = y * 2 + c
    row = z * 4 + x

    barrier = pltpu.get_barrier_semaphore()

    def greet_col(d, _):
        p = lax.rem(col + d, 8)
        pl.semaphore_signal(barrier, inc=1, device_id=(z, x, lax.div(p, 2), lax.rem(p, 2)), device_id_type=MESH)
        return 0

    def greet_row(d, _):
        p = lax.rem(row + d, 16)
        pl.semaphore_signal(barrier, inc=1, device_id=(lax.div(p, 4), lax.rem(p, 4), y, c), device_id_type=MESH)
        return 0

    lax.fori_loop(1, 8, greet_col, 0)
    lax.fori_loop(1, 16, greet_row, 0)
    pl.semaphore_wait(barrier, 22)

    def remote(src, dst, ss, rs, dev):
        return pltpu.make_async_remote_copy(
            src_ref=src, dst_ref=dst, send_sem=ss, recv_sem=rs, device_id=dev, device_id_type=MESH
        )

    ydev = [(z, x, ym, c), (z, x, yp, c)]
    xdev = [(z, xm, y, c), (z, xp, y, c)]
    zdev = [(zm, x, y, c), (zp, x, y, c)]
    sdev = (z, x, y, sib)

    def rows_of(yy, cc):
        return pl.ds(pl.multiple_of((yy * 2 + cc) * SLAB, SLAB), SLAB)

    mine = rows_of(y, c)

    def extra(src_chunk, slot, direction, k):
        return remote(
            inp.at[:, pl.ds(src_chunk * CH, CH)], IN.at[OWN + slot, mine], sx.at[k], rx.at[slot], xdev[direction]
        )

    @pl.when(x == 1)
    def _():
        extra(0, 0, MINUS, 0).start()
        extra(5, 0, PLUS, 1).start()
        extra(6, 1, PLUS, 2).start()

    @pl.when(x == 2)
    def _():
        extra(6, 0, PLUS, 0).start()
        extra(0, 0, MINUS, 1).start()
        extra(1, 1, MINUS, 2).start()

    def grow(zz, xx):
        return pl.ds(pl.multiple_of((zz * 4 + xx) * GS, GS), GS)

    def gpart(zz, xx, part):
        return pl.ds(pl.multiple_of((zz * 4 + xx) * GS + part * (GS // 2), GS // 2), GS // 2)

    first_dev = [xdev, zdev]
    second_dev = [zdev, xdev]

    def along_first(h, d):
        if h == 0:
            return (z, [x, xm, xp, xf][d])
        return ([z, zm, zp, zf][d], x)

    def second_of(h, slot, d):
        zz, xx = along_first(h, slot)
        if h == 0:
            return ([z, zm, zp, zf][d], xx)
        return (zz, [x, xm, xp, xf][d])

    def first_send(h, direction):
        r = grow(z, x)
        return remote(
            og.at[:, pl.ds(h * HALF, HALF)], OG.at[h, r], oa1s.at[h, direction], oa1r.at[h, 1 - direction],
            first_dev[h][direction],
        )

    def first_wait(h, frm):
        r = grow(*along_first(h, 1 + frm))
        remote(OG.at[h, r], OG.at[h, r], oa1s.at[h, frm], oa1r.at[h, frm], first_dev[h][frm]).wait_recv()

    def first_forward(h, frm):
        r = gpart(*along_first(h, 1 + frm), frm)
        return remote(
            OG.at[h, r], OG.at[h, r], of1s.at[h, frm], of1r.at[h, frm], first_dev[h][1 - frm]
        )

    def first_far_wait(h, frm):
        r = gpart(*along_first(h, 3), frm)
        remote(OG.at[h, r], OG.at[h, r], of1s.at[h, frm], of1r.at[h, frm], first_dev[h][frm]).wait_recv()

    def second_send(h, slot, direction):
        r = grow(*along_first(h, slot))
        src = og.at[:, pl.ds(h * HALF, HALF)] if slot == 0 else OG.at[h, r]
        return remote(
            src, OG.at[h, r], oa2s.at[h, slot, direction], oa2r.at[h, slot, 1 - direction], second_dev[h][direction]
        )

    def second_wait(h, slot, frm):
        r = grow(*second_of(h, slot, 1 + frm))
        remote(
            OG.at[h, r], OG.at[h, r], oa2s.at[h, slot, frm], oa2r.at[h, slot, frm], second_dev[h][frm]
        ).wait_recv()

    def second_forward(h, slot, frm):
        r = gpart(*second_of(h, slot, 1 + frm), frm)
        return remote(
            OG.at[h, r], OG.at[h, r], of2s.at[h, slot, frm], of2r.at[h, slot, frm], second_dev[h][1 - frm]
        )

    def second_far_wait(h, slot, frm):
        r = gpart(*second_of(h, slot, 3), frm)
        remote(
            OG.at[h, r], OG.at[h, r], of2s.at[h, slot, frm], of2r.at[h, slot, frm], second_dev[h][frm]
        ).wait_recv()

    for h in (0, 1):
        for d in (MINUS, PLUS):
            first_send(h, d).start()
    for h in (0, 1):
        for d in (MINUS, PLUS):
            second_send(h, 0, d).start()

    def own_src(k):
        return inp.at[:, pl.ds(pl.multiple_of(k * CH, CH), CH)]

    def y_send(src, k, direction):
        return remote(src, IN.at[k, mine], sy.at[direction, k], ry.at[1 - direction, k], ydev[direction])

    def relay(src, kind, k, yy):
        return remote(src, IN.at[k, rows_of(yy, c)], sb.at[kind, k], rb.at[kind, k], sdev)

    def local(k):
        return pltpu.make_async_copy(own_src(k), IN.at[k, mine], lc.at[k])

    def start_own(k, _):
        y_send(own_src(k), k, MINUS).start()
        y_send(own_src(k), k, PLUS).start()
        return 0

    lax.fori_loop(0, OWN, start_own, 0)

    def start_near(k, _):
        local(k).start()
        relay(own_src(k), 0, k, y).start()
        return 0

    lax.fori_loop(0, OWN, start_near, 0)

    def og_local(h):
        return pltpu.make_async_copy(og.at[:, pl.ds(h * HALF, HALF)], OG.at[h, grow(z, x)], ol.at[h])

    og_local(0).start()
    og_local(1).start()

    def start_extra(k, _):
        slot = k - OWN
        src = IN.at[k, mine]
        remote(src, src, sx.at[0], rx.at[slot], xdev[0]).wait_recv()
        y_send(src, k, MINUS).start()
        y_send(src, k, PLUS).start()
        relay(src, 0, k, y).start()
        return 0

    lax.fori_loop(OWN, nch, start_extra, 0)

    for h in (1, 0):
        for frm in (MINUS, PLUS):
            first_wait(h, frm)
            first_forward(h, frm).start()
            for d in (MINUS, PLUS):
                second_send(h, 1 + frm, d).start()
    for h in (1, 0):
        for frm in (MINUS, PLUS):
            second_wait(h, 0, frm)
            second_forward(h, 0, frm).start()
    for h in (1, 0):
        for frm in (MINUS, PLUS):
            first_far_wait(h, frm)
        for d in (MINUS, PLUS):
            second_send(h, 3, d).start()
    for slot in (1, 2, 3):
        for h in (1, 0):
            for frm in (MINUS, PLUS):
                second_wait(h, slot, frm)
                second_forward(h, slot, frm).start()

    def y_wait(k, frm):
        r = IN.at[k, rows_of([ym, yp][frm], c)]
        remote(r, r, sy.at[frm, k], ry.at[frm, k], ydev[frm]).wait_recv()

    def y_forward(k, frm):
        r = IN.at[k, rows_of([ym, yp][frm], c)]
        return remote(r, r, sf.at[k], rf.at[k], ydev[1 - frm])

    def y_far_wait(k):
        r = IN.at[k, rows_of(yf, c)]
        remote(r, r, sf.at[k], rf.at[k], ydev[0]).wait_recv()

    def relay_wait(kind, k, yy):
        r = IN.at[k, rows_of(yy, sib)]
        remote(r, r, sb.at[kind, k], rb.at[kind, k], sdev).wait_recv()

    def middle(k, _):
        for frm in (MINUS, PLUS):
            y_wait(k, frm)

            @pl.when(lax.rem(k, 2) == frm)
            def _():
                y_forward(k, frm).start()

            relay(IN.at[k, rows_of([ym, yp][frm], c)], 1 + frm, k, [ym, yp][frm]).start()
        return 0

    lax.fori_loop(0, nch, middle, 0)

    for slot in (0, 1, 2, 3):
        for h in (1, 0):
            for frm in (MINUS, PLUS):
                second_far_wait(h, slot, frm)
    og_local(0).wait()
    og_local(1).wait()

    def local_wait(k, _):
        local(k).wait()
        return 0

    lax.fori_loop(0, OWN, local_wait, 0)

    def weight(m):
        one = uids[m].astype(jnp.float32)
        return 1.0 - one, one

    def mb_rows(m):
        return pl.ds(pl.multiple_of(m * MB, MB), MB)

    near = [y, ym, yp]
    near_w = [weight(m) for m in near]

    def near_grads(k, _):
        relay_wait(0, k, y)
        relay_wait(1, k, ym)
        relay_wait(2, k, yp)
        for h in (0, 1):
            cols = slice(h * HALF, (h + 1) * HALF)
            zero = one = None
            for m, (w0, w1) in zip(near, near_w):
                p = dot_tn(IN[k, mb_rows(m)], OG[h, mb_rows(m)])
                zero = p * w0 if zero is None else zero + p * w0
                one = p * w1 if one is None else one + p * w1
            ACC[k, 0, :, cols] = zero
            ACC[k, 1, :, cols] = one
        return 0

    lax.fori_loop(0, nch, near_grads, 0)

    far_w = weight(yf)
    SQ[...] = jnp.zeros_like(SQ)

    def far_grads(k):
        relay_wait(3, k, yf)
        counts = jnp.where(k < OWN, 1.0, 0.0)
        for h in (0, 1):
            cols = slice(h * HALF, (h + 1) * HALF)
            p = dot_tn(IN[k, mb_rows(yf)], OG[h, mb_rows(yf)])
            for u in (0, 1):
                g = (ACC[k, u, :, cols] + p * far_w[u]).astype(jnp.bfloat16)
                G[k, u, :, cols] = g
                wide = g.astype(jnp.float32)
                SQ[u : u + 1, cols] += jnp.sum(wide * wide, axis=0, keepdims=True) * counts

    def far(k, _):
        y_far_wait(k)
        relay(IN.at[k, rows_of(yf, c)], 3, k, yf).start()

        @pl.when(k > 0)
        def _():
            far_grads(k - 1)

        return 0

    lax.fori_loop(0, nch, far, 0)
    far_grads(nch - 1)

    sums = jnp.zeros((8, 128), jnp.float32)
    for j in range(8):
        sums = sums + SQ[:, j * 128 : (j + 1) * 128]
    S1[...] = sums

    def col_copy(d):
        p = lax.rem(col + d, 8)
        return remote(S1, R1.at[col], a1s.at[d], a1r.at[col], (z, x, lax.div(p, 2), lax.rem(p, 2)))

    def col_start(d, _):
        col_copy(d).start()
        return 0

    def col_wait(d, _):
        p = lax.rem(col + d, 8)
        remote(S1, R1.at[p], a1s.at[d], a1r.at[p], sdev).wait_recv()
        return 0

    lax.fori_loop(1, 8, col_start, 0)
    R1[col] = S1[...]
    lax.fori_loop(1, 8, col_wait, 0)
    total = R1[0]
    for j in range(1, 8):
        total = total + R1[j]
    S2[...] = total

    def row_copy(d):
        p = lax.rem(row + d, 16)
        return remote(S2, R2.at[row], a2s.at[d], a2r.at[row], (lax.div(p, 4), lax.rem(p, 4), y, c))

    def row_start(d, _):
        row_copy(d).start()
        return 0

    def row_wait(d, _):
        p = lax.rem(row + d, 16)
        remote(S2, R2.at[p], a2s.at[d], a2r.at[p], sdev).wait_recv()
        return 0

    lax.fori_loop(1, 16, row_start, 0)
    R2[row] = S2[...]
    lax.fori_loop(1, 16, row_wait, 0)
    total = R2[0]
    for j in range(1, 16):
        total = total + R2[j]
    factor = TARGET / jnp.sqrt(jnp.sum(total, axis=1, keepdims=True) + 1e-06)
    f0 = factor[0:1, :]
    f1 = factor[1:2, :]

    right = x >= 2
    s1 = jnp.where(inner, 8, jnp.where(right, 0, 4))
    s2 = jnp.where(right, jnp.where(inner, 0, 1), 5)
    shared = [jnp.int32(7), s1, s2, s2 + 1]

    def out_copy(t, i, q):
        return pltpu.make_async_copy(
            OUTB.at[t * 4 + i], out.at[pl.ds(pl.multiple_of(q * CH, CH), CH)], od.at[t * 4 + i]
        )

    def give_back(direction):
        q = 0 if direction == PLUS else OWN - 1
        return remote(OUTB.at[0], out.at[pl.ds(q * CH, CH)], ret_s, ret_r, xdev[direction])

    def chunk_of(t, i):
        return jnp.where(t == 0, shared[i], x + i)

    def task(t, _):
        for i in range(4):
            q = chunk_of(t, i)
            X[i * CH : (i + 1) * CH] = (
                f0 * G[q, 0].astype(jnp.float32) + f1 * G[q, 1].astype(jnp.float32)
            ).astype(jnp.bfloat16)
        for i in range(4):
            r = slice(i * CH, (i + 1) * CH)
            A[r] = dot_nt(X[r], X[...]).astype(jnp.bfloat16)
        for i in range(4):
            r = slice(i * CH, (i + 1) * CH)
            X1[r] = (1.5 * X[r].astype(jnp.float32) - 0.5 * dot_nn(A[r], X[...])).astype(jnp.bfloat16)

        def last(i):
            r = slice(i * CH, (i + 1) * CH)
            gram = dot_nt(X1[r], X1[...]).astype(jnp.bfloat16)
            done = (1.5 * X1[r].astype(jnp.float32) - 0.5 * dot_nn(gram, X1[...])) * LAST_SCALE
            OUTB[t * 4 + i] = done.astype(jnp.bfloat16)

        outer_or_whole = jnp.logical_or(t == 1, jnp.logical_not(inner))

        @pl.when(outer_or_whole)
        def _():
            last(0)

        @pl.when(jnp.logical_and(t == 0, x == 0))
        def _():
            give_back(PLUS).start()

        @pl.when(jnp.logical_and(t == 0, x == 3))
        def _():
            give_back(MINUS).start()

        @pl.when(t == 1)
        def _():
            out_copy(t, 0, chunk_of(t, 0)).start()

        @pl.when(outer_or_whole)
        def _():
            last(1)
            out_copy(t, 1, chunk_of(t, 1)).start()

        for i in (2, 3):
            last(i)
            out_copy(t, i, chunk_of(t, i)).start()
        return 0

    lax.fori_loop(0, 2, task, 0)

    for t in (0, 1):
        for i in range(4):
            if t == 0 and i == 0:
                continue
            if t == 0 and i == 1:

                @pl.when(jnp.logical_not(inner))
                def _():
                    out_copy(0, 1, chunk_of(0, 1)).wait()

                continue
            out_copy(t, i, chunk_of(t, i)).wait()

    @pl.when(x == 0)
    def _():
        give_back(PLUS).wait_send()

    @pl.when(x == 3)
    def _():
        give_back(MINUS).wait_send()

    @pl.when(x == 1)
    def _():
        give_back(PLUS).wait_recv()

    @pl.when(x == 2)
    def _():
        give_back(MINUS).wait_recv()

    @pl.when(inner)
    def _():
        for k in range(3):
            extra(0, 0, MINUS, k).wait_send()

    for h in (0, 1):
        for d in (MINUS, PLUS):
            first_send(h, d).wait_send()
            first_forward(h, d).wait_send()
            for slot in range(4):
                second_send(h, slot, d).wait_send()
                second_forward(h, slot, d).wait_send()

    def drain(k, _):
        src = IN.at[k, mine]
        y_send(src, k, MINUS).wait_send()
        y_send(src, k, PLUS).wait_send()
        y_forward(k, MINUS).wait_send()
        for kind in range(4):
            relay(src, kind, k, y).wait_send()
        return 0

    lax.fori_loop(0, nch, drain, 0)

    def drain_col(d, _):
        col_copy(d).wait_send()
        return 0

    def drain_row(d, _):
        row_copy(d).wait_send()
        return 0

    lax.fori_loop(1, 8, drain_col, 0)
    lax.fori_loop(1, 16, drain_row, 0)


def per_device(inputs, out_grads, user_ids):
    dma = pltpu.SemaphoreType.DMA
    n = OWN + 2
    bf16, f32 = jnp.bfloat16, jnp.float32
    return pl.pallas_call(
        kernel,
        out_shape=jax.ShapeDtypeStruct((OWN * CH, BLOCK), bf16),
        in_specs=[
            pl.BlockSpec(memory_space=pltpu.SMEM),
            pl.BlockSpec(memory_space=pl.ANY),
            pl.BlockSpec(memory_space=pl.ANY),
        ],
        out_specs=pl.BlockSpec(memory_space=pl.ANY),
        scratch_shapes=[
            pltpu.VMEM((n, 4 * MB, CH), bf16),
            pltpu.VMEM((2, 4 * MB, HALF), bf16),
            pltpu.VMEM((n, 2, CH, BLOCK), f32),
            pltpu.VMEM((n, 2, CH, BLOCK), bf16),
            pltpu.VMEM((BLOCK, BLOCK), bf16),
            pltpu.VMEM((BLOCK, BLOCK), bf16),
            pltpu.VMEM((BLOCK, BLOCK), bf16),
            pltpu.VMEM((8, CH, BLOCK), bf16),
            pltpu.VMEM((8, BLOCK), f32),
            pltpu.VMEM((8, 128), f32),
            pltpu.VMEM((8, 8, 128), f32),
            pltpu.VMEM((8, 128), f32),
            pltpu.VMEM((16, 8, 128), f32),
            dma((2, n)), dma((2, n)), dma((n,)), dma((n,)), dma((4, n)), dma((4, n)), dma((n,)), dma((3,)), dma((2,)),
            dma((2, 2)), dma((2, 2)), dma((2, 2)), dma((2, 2)),
            dma((2, 4, 2)), dma((2, 4, 2)), dma((2, 4, 2)), dma((2, 4, 2)), dma((2,)),
            dma((8,)), dma((8,)), dma((16,)), dma((16,)), dma, dma, dma((8,)),
        ],
        compiler_params=pltpu.CompilerParams(
            collective_id=0, has_side_effects=True, vmem_limit_bytes=60 * 1024 * 1024
        ),
    )(user_ids, inputs, out_grads)


def solution(mesh):
    torus = Mesh(mesh.devices.reshape(4, 4, 4, 2), ("z", "x", "y", "c"))
    return jax.shard_map(
        per_device,
        mesh=torus,
        in_specs=(P(("y", "c"), ("z", "x")), P(("z", "x"), ("y", "c")), P()),
        out_specs=P(("z", "x"), ("y", "c")),
        check_vma=False,
    )
```

```python
import math

import jax
import jax.numpy as jnp
from jax import lax
from jax.experimental import pallas as pl
from jax.experimental.pallas import tpu as pltpu
from jax.sharding import Mesh
from jax.sharding import PartitionSpec as P

FF = 28672
D = 8192
BLOCK = 1024
TARGET = 0.15 * math.sqrt(FF * D / BLOCK)
LAST_SCALE = math.sqrt(BLOCK)

MESH = pl.DeviceIdType.MESH
CH = 256
OWN = 7
SLAB = 192
MB = 384
GS = 96
HALF = 512
MINUS, PLUS = 0, 1


def dot_tn(a, b):
    return lax.dot_general(a, b, (((0,), (0,)), ((), ())), preferred_element_type=jnp.float32)


def dot_nt(a, b):
    return lax.dot_general(a, b, (((1,), (1,)), ((), ())), preferred_element_type=jnp.float32)


def dot_nn(a, b):
    return lax.dot_general(a, b, (((1,), (0,)), ((), ())), preferred_element_type=jnp.float32)


def kernel(
    uids, inp, og, out,
    NEAR, FAR, XNEAR, XFAR, OG, G, X, X1, A, BACK, SQ, S1, R1, S2, R2,
    sy, ry, sf, rf, sh, rh, sb, rb, lc, sx, rx,
    oa1s, oa1r, of1s, of1r, oa2s, oa2r, of2s, of2r, ol,
    a1s, a1r, a2s, a2r, ret_s, ret_r,
):
    z, x, y, c = (lax.axis_index(a) for a in ("z", "x", "y", "c"))
    zm, zp, zf = (lax.rem(z + d, 4) for d in (3, 1, 2))
    xm, xp, xf = (lax.rem(x + d, 4) for d in (3, 1, 2))
    ym, yp, yf = (lax.rem(y + d, 4) for d in (3, 1, 2))
    sib = 1 - c
    inner = jnp.logical_or(x == 1, x == 2)
    extras = jnp.where(inner, 2, 1)
    col = y * 2 + c
    row = z * 4 + x

    barrier = pltpu.get_barrier_semaphore()
    for dev in ((z, x, ym, c), (z, x, yp, c), (z, xm, y, c), (z, xp, y, c), (zm, x, y, c), (zp, x, y, c), (z, x, y, sib)):
        pl.semaphore_signal(barrier, inc=1, device_id=dev, device_id_type=MESH)
    pl.semaphore_wait(barrier, 7)

    def remote(src, dst, ss, rs, dev):
        return pltpu.make_async_remote_copy(
            src_ref=src, dst_ref=dst, send_sem=ss, recv_sem=rs, device_id=dev, device_id_type=MESH
        )

    ydev = [(z, x, ym, c), (z, x, yp, c)]
    xdev = [(z, xm, y, c), (z, xp, y, c)]
    zdev = [(zm, x, y, c), (zp, x, y, c)]
    sdev = (z, x, y, sib)

    def slab(cc):
        return pl.ds(pl.multiple_of(cc * SLAB, SLAB), SLAB)

    def extra(src_chunk, slot, direction, k):
        return remote(
            inp.at[:, pl.ds(src_chunk * CH, CH)], XNEAR.at[slot, 0, slab(c)], sx.at[k], rx.at[slot], xdev[direction]
        )

    def start_shared():
        @pl.when(x == 1)
        def _():
            extra(5, 0, PLUS, 0).start()
            extra(0, 0, MINUS, 1).start()
            extra(6, 1, PLUS, 2).start()

        @pl.when(x == 2)
        def _():
            extra(0, 0, MINUS, 0).start()
            extra(6, 0, PLUS, 1).start()
            extra(1, 1, MINUS, 2).start()

    def grow(zz, xx):
        return zz, pl.ds(pl.multiple_of(xx * GS, GS), GS)

    def gpart(zz, xx, part):
        return zz, pl.ds(pl.multiple_of(xx * GS + part * (GS // 2), GS // 2), GS // 2)

    first_dev = [xdev, zdev]
    second_dev = [zdev, xdev]

    def along_first(h, d):
        if h == 0:
            return (z, [x, xm, xp, xf][d])
        return ([z, zm, zp, zf][d], x)

    def second_of(h, slot, d):
        zz, xx = along_first(h, slot)
        if h == 0:
            return ([z, zm, zp, zf][d], xx)
        return (zz, [x, xm, xp, xf][d])

    def first_send(h, direction):
        r = grow(z, x)
        return remote(
            og.at[:, pl.ds(h * HALF, HALF)], OG.at[h, r[0], r[1]], oa1s.at[h, direction], oa1r.at[h, 1 - direction],
            first_dev[h][direction],
        )

    def first_wait(h, frm):
        r = grow(*along_first(h, 1 + frm))
        remote(OG.at[h, r[0], r[1]], OG.at[h, r[0], r[1]], oa1s.at[h, frm], oa1r.at[h, frm], first_dev[h][frm]).wait_recv()

    def first_forward(h, frm):
        r = gpart(*along_first(h, 1 + frm), frm)
        return remote(
            OG.at[h, r[0], r[1]], OG.at[h, r[0], r[1]], of1s.at[h, frm], of1r.at[h, frm], first_dev[h][1 - frm]
        )

    def first_far_wait(h, frm):
        r = gpart(*along_first(h, 3), frm)
        remote(OG.at[h, r[0], r[1]], OG.at[h, r[0], r[1]], of1s.at[h, frm], of1r.at[h, frm], first_dev[h][frm]).wait_recv()

    def second_send(h, slot, direction):
        r = grow(*along_first(h, slot))
        src = og.at[:, pl.ds(h * HALF, HALF)] if slot == 0 else OG.at[h, r[0], r[1]]
        return remote(
            src, OG.at[h, r[0], r[1]], oa2s.at[h, slot, direction], oa2r.at[h, slot, 1 - direction], second_dev[h][direction]
        )

    def second_wait(h, slot, frm):
        r = grow(*second_of(h, slot, 1 + frm))
        remote(
            OG.at[h, r[0], r[1]], OG.at[h, r[0], r[1]], oa2s.at[h, slot, frm], oa2r.at[h, slot, frm], second_dev[h][frm]
        ).wait_recv()

    def second_forward(h, slot, frm):
        r = gpart(*second_of(h, slot, 1 + frm), frm)
        return remote(
            OG.at[h, r[0], r[1]], OG.at[h, r[0], r[1]], of2s.at[h, slot, frm], of2r.at[h, slot, frm], second_dev[h][1 - frm]
        )

    def second_far_wait(h, slot, frm):
        r = gpart(*second_of(h, slot, 3), frm)
        remote(
            OG.at[h, r[0], r[1]], OG.at[h, r[0], r[1]], of2s.at[h, slot, frm], of2r.at[h, slot, frm], second_dev[h][frm]
        ).wait_recv()

    for h in (0, 1):
        for d in (MINUS, PLUS):
            first_send(h, d).start()
    for h in (0, 1):
        for d in (MINUS, PLUS):
            second_send(h, 0, d).start()

    place_of = (2, 1)

    def own_src(k):
        return inp.at[:, pl.ds(pl.multiple_of(k * CH, CH), CH)]

    def y_send(src, buf, k, g, direction):
        return remote(
            src, buf.at[k, place_of[1 - direction], slab(c)], sy.at[direction, g], ry.at[1 - direction, g], ydev[direction]
        )

    def y_wait(buf, k, g, frm):
        r = buf.at[k, place_of[frm], slab(c)]
        remote(r, r, sy.at[frm, g], ry.at[frm, g], ydev[frm]).wait_recv()

    def y_forward(buf, dst, k, g, frm):
        return remote(
            buf.at[k, place_of[frm], slab(c)], dst.at[k, slab(c)], sf.at[g], rf.at[g], ydev[1 - frm]
        )

    def split_forward(frm):
        k = OWN - 1
        part = pl.ds(pl.multiple_of(c * SLAB + frm * (SLAB // 2), SLAB // 2), SLAB // 2)
        return remote(NEAR.at[k, place_of[frm], part], FAR.at[k, part], sh.at[frm], rh.at[frm], ydev[1 - frm])

    def y_far_wait(dst, k, g):
        r = dst.at[k, slab(c)]
        remote(r, r, sf.at[g], rf.at[g], ydev[0]).wait_recv()

    def relay(src, dst, k, g, kind):
        r = slab(c)
        return remote(src, dst.at[k, r] if kind == 3 else dst.at[k, (0, 2, 1)[kind], r], sb.at[kind, g], rb.at[kind, g], sdev)

    def relay_wait(dst, k, g, kind):
        r = slab(sib)
        r = dst.at[k, r] if kind == 3 else dst.at[k, (0, 2, 1)[kind], r]
        remote(r, r, sb.at[kind, g], rb.at[kind, g], sdev).wait_recv()

    def local(k):
        return pltpu.make_async_copy(own_src(k), NEAR.at[k, 0, slab(c)], lc.at[k])

    def start_own(k, _):
        y_send(own_src(k), NEAR, k, k, MINUS).start()
        y_send(own_src(k), NEAR, k, k, PLUS).start()
        return 0

    lax.fori_loop(0, OWN, start_own, 0)

    def og_local(h):
        return pltpu.make_async_copy(og.at[:, pl.ds(h * HALF, HALF)], OG.at[(h, *grow(z, x))], ol.at[h])

    og_local(0).start()
    og_local(1).start()

    def start_near(k, _):
        local(k).start()
        relay(own_src(k), NEAR, k, k, 0).start()
        return 0

    lax.fori_loop(0, OWN, start_near, 0)

    for h in (1, 0):
        for frm in (MINUS, PLUS):
            first_wait(h, frm)
            first_forward(h, frm).start()
            for d in (MINUS, PLUS):
                second_send(h, 1 + frm, d).start()
    for h in (1, 0):
        for frm in (MINUS, PLUS):
            second_wait(h, 0, frm)
            second_forward(h, 0, frm).start()
    for h in (1, 0):
        for frm in (MINUS, PLUS):
            first_far_wait(h, frm)
        for d in (MINUS, PLUS):
            second_send(h, 3, d).start()
    for slot in (1, 2, 3):
        for h in (1, 0):
            for frm in (MINUS, PLUS):
                second_wait(h, slot, frm)
                second_forward(h, slot, frm).start()

    start_shared()

    def middle(k, _):
        for frm in (MINUS, PLUS):
            y_wait(NEAR, k, k, frm)

            @pl.when(jnp.logical_and(lax.rem(k, 2) == frm, k < OWN - 1))
            def _():
                y_forward(NEAR, FAR, k, k, frm).start()

            relay(NEAR.at[k, place_of[frm], slab(c)], NEAR, k, k, 1 + frm).start()
        return 0

    lax.fori_loop(0, OWN, middle, 0)
    split_forward(MINUS).start()
    split_forward(PLUS).start()

    for slot in (0, 1, 2, 3):
        for h in (1, 0):
            for frm in (MINUS, PLUS):
                second_far_wait(h, slot, frm)
    og_local(0).wait()
    og_local(1).wait()

    def near_wait(k, _):
        local(k).wait()
        for kind in (0, 1, 2):
            relay_wait(NEAR, k, k, kind)
        return 0

    lax.fori_loop(0, OWN, near_wait, 0)

    user_far = uids[yf]
    d1 = lax.rem(uids[yp] + user_far, 2)
    d2 = lax.rem(uids[ym] + user_far, 2)
    near_hit = (1 - d1) + 2 * d1 * (1 - d2)
    near_a = 1 - jnp.minimum(near_hit, 1)
    near_b = 2 - lax.div(near_hit, 2)

    def og_mb(place):
        return lax.rem(y + place + lax.div(place, 2), 4)

    mb_hit, mb_a, mb_b = og_mb(near_hit), og_mb(near_a), og_mb(near_b)
    SQ[...] = jnp.zeros_like(SQ)

    def grads(near, far, k, q, u, counted):
        for h in (0, 1):
            cols = slice(h * HALF, (h + 1) * HALF)
            if u == 1:
                p = dot_tn(near[k, near_a], OG[h, mb_a])
                p = p + dot_tn(near[k, near_b], OG[h, mb_b])
            else:
                p = dot_tn(near[k, near_hit], OG[h, mb_hit])
                p = p + dot_tn(far[k], OG[h, yf])
            G[q, u, :, cols] = p.astype(jnp.bfloat16)
            if counted:
                SQ[u : u + 1, cols] += jnp.sum(p * p, axis=0, keepdims=True)

    def far_relay(k):
        if k == OWN - 1:
            for frm in (MINUS, PLUS):
                part = pl.ds(pl.multiple_of(c * SLAB + frm * (SLAB // 2), SLAB // 2), SLAB // 2)
                r = FAR.at[k, part]
                remote(r, r, sh.at[frm], rh.at[frm], ydev[frm]).wait_recv()
        else:
            y_far_wait(FAR, k, k)
        relay(FAR.at[k, slab(c)], FAR, k, k, 3).start()

    def start_extra(slot, _):
        src = XNEAR.at[slot, 0, slab(c)]
        g = OWN + slot
        remote(src, src, sx.at[0], rx.at[slot], xdev[0]).wait_recv()
        y_send(src, XNEAR, slot, g, MINUS).start()
        y_send(src, XNEAR, slot, g, PLUS).start()
        relay(src, XNEAR, slot, g, 0).start()
        return 0

    for k in range(OWN):
        grads(NEAR, FAR, k, k, 1, True)
        far_relay(k)
        if k == 2:
            lax.fori_loop(0, extras, start_extra, 0)
    for k in range(OWN):
        relay_wait(FAR, k, k, 3)
        grads(NEAR, FAR, k, k, 0, True)

    far_one = user_far.astype(jnp.float32)
    far_zero = 1.0 - far_one
    sums = jnp.zeros((8, 128), jnp.float32)
    for j in range(8):
        sums = sums + SQ[:, j * 128 : (j + 1) * 128]
    S2[...] = jnp.zeros_like(S2)
    S2[0:1] = sums[0:1] * far_zero + sums[1:2] * far_one
    S2[1:2] = sums[0:1] * far_one + sums[1:2] * far_zero

    def row_copy(d):
        p = lax.rem(row + d, 16)
        return remote(S2, R2.at[row], a2s.at[d], a2r.at[row], (lax.div(p, 4), lax.rem(p, 4), y, c))

    def row_start(d, _):
        row_copy(d).start()
        return 0

    def row_wait(d, _):
        p = lax.rem(row + d, 16)
        remote(S2, R2.at[p], a2s.at[d], a2r.at[p], sdev).wait_recv()
        return 0

    lax.fori_loop(1, 16, row_start, 0)
    R2[row] = S2[...]

    def extra_middle(slot, _):
        g = OWN + slot
        for frm in (MINUS, PLUS):
            y_wait(XNEAR, slot, g, frm)

            @pl.when(slot == frm)
            def _():
                y_forward(XNEAR, XFAR, slot, g, frm).start()

            relay(XNEAR.at[slot, place_of[frm], slab(c)], XNEAR, slot, g, 1 + frm).start()
        return 0

    lax.fori_loop(0, extras, extra_middle, 0)
    lax.fori_loop(1, 16, row_wait, 0)
    total = R2[0]
    for j in range(1, 16):
        total = total + R2[j]
    S1[...] = total

    def col_copy(d):
        p = lax.rem(col + d, 8)
        return remote(S1, R1.at[col], a1s.at[d], a1r.at[col], (z, x, lax.div(p, 2), lax.rem(p, 2)))

    def col_start(d, _):
        col_copy(d).start()
        return 0

    def col_wait(d, _):
        p = lax.rem(col + d, 8)
        remote(S1, R1.at[p], a1s.at[d], a1r.at[p], sdev).wait_recv()
        return 0

    lax.fori_loop(1, 8, col_start, 0)
    R1[col] = S1[...]

    def extra_far(slot, _):
        g = OWN + slot
        y_far_wait(XFAR, slot, g)
        relay(XFAR.at[slot, slab(c)], XFAR, slot, g, 3).start()
        return 0

    def extra_near_wait(slot, _):
        for kind in (0, 1, 2, 3):
            relay_wait(XFAR if kind == 3 else XNEAR, slot, OWN + slot, kind)
        return 0

    lax.fori_loop(0, extras, extra_far, 0)
    lax.fori_loop(0, extras, extra_near_wait, 0)

    def extra_grads(slot, _):
        grads(XNEAR, XFAR, slot, OWN + slot, 1, False)
        grads(XNEAR, XFAR, slot, OWN + slot, 0, False)
        return 0

    lax.fori_loop(0, extras, extra_grads, 0)
    lax.fori_loop(1, 8, col_wait, 0)
    total = R1[0]
    for j in range(1, 8):
        total = total + R1[j]
    factor = TARGET / jnp.sqrt(jnp.sum(total, axis=1, keepdims=True) + 1e-06)
    f_hit = factor[0:1, :] * far_zero + factor[1:2, :] * far_one
    f_other = factor[0:1, :] * far_one + factor[1:2, :] * far_zero

    right = x >= 2
    s1 = jnp.where(inner, 8, jnp.where(right, 0, 4))
    s2 = jnp.where(right, jnp.where(inner, 0, 1), 5)
    shared = [jnp.int32(7), s1, s2, s2 + 1]

    def give_back(direction):
        q = 0 if direction == PLUS else OWN - 1
        return remote(BACK, out.at[pl.ds(q * CH, CH)], ret_s, ret_r, xdev[direction])

    def chunk_of(t, i):
        return jnp.where(t == 0, shared[i], x + i)

    def gram_rows(src, i):
        r = slice(i * CH, (i + 1) * CH)
        t = dot_nt(src[r], src[i * CH :]).astype(jnp.bfloat16)
        A[r, i * CH :] = t
        for j in range(i + 1, 4):
            A[j * CH : (j + 1) * CH, r] = t[:, (j - i) * CH : (j - i + 1) * CH].T

    def finish(rows, gram):
        done = (1.5 * rows.astype(jnp.float32) - 0.5 * dot_nn(gram, X1[...])) * LAST_SCALE
        return done.astype(jnp.bfloat16)

    def put(t, i, value):
        out[pl.ds(pl.multiple_of(chunk_of(t, i) * CH, CH), CH)] = value

    def task(t, _):
        for i in range(4):
            q = chunk_of(t, i)
            X[i * CH : (i + 1) * CH] = (
                f_hit * G[q, 0].astype(jnp.float32) + f_other * G[q, 1].astype(jnp.float32)
            ).astype(jnp.bfloat16)
        for i in range(4):
            gram_rows(X, i)
        for i in range(4):
            r = slice(i * CH, (i + 1) * CH)
            X1[r] = (1.5 * X[r].astype(jnp.float32) - 0.5 * dot_nn(A[r], X[...])).astype(jnp.bfloat16)

        half = jnp.logical_and(t == 0, inner)

        @pl.when(half)
        def _():
            for i in (2, 3):
                r = slice(i * CH, (i + 1) * CH)
                put(t, i, finish(X1[r], dot_nt(X1[r], X1[...]).astype(jnp.bfloat16)))

        @pl.when(jnp.logical_not(half))
        def _():
            gram_rows(X1, 0)
            first = finish(X1[0:CH], A[0:CH])

            @pl.when(t == 0)
            def _():
                BACK[...] = first

                @pl.when(x == 0)
                def _():
                    give_back(PLUS).start()

                @pl.when(x == 3)
                def _():
                    give_back(MINUS).start()

            @pl.when(t == 1)
            def _():
                put(t, 0, first)

            for i in (1, 2, 3):
                gram_rows(X1, i)
            for i in (1, 2, 3):
                r = slice(i * CH, (i + 1) * CH)
                put(t, i, finish(X1[r], A[r]))

        return 0

    lax.fori_loop(0, 2, task, 0)

    @pl.when(x == 0)
    def _():
        give_back(PLUS).wait_send()

    @pl.when(x == 3)
    def _():
        give_back(MINUS).wait_send()

    @pl.when(x == 1)
    def _():
        give_back(PLUS).wait_recv()

    @pl.when(x == 2)
    def _():
        give_back(MINUS).wait_recv()

    @pl.when(inner)
    def _():
        for k in range(3):
            extra(0, 0, MINUS, k).wait_send()

    for h in (0, 1):
        for d in (MINUS, PLUS):
            first_send(h, d).wait_send()
            first_forward(h, d).wait_send()
            for slot in range(4):
                second_send(h, slot, d).wait_send()
                second_forward(h, slot, d).wait_send()

    def drain(k, _):
        for d in (MINUS, PLUS):
            y_send(own_src(k), NEAR, k, k, d).wait_send()
        for kind in range(4):
            relay(own_src(k), FAR if kind == 3 else NEAR, k, k, kind).wait_send()

        @pl.when(k < OWN - 1)
        def _():
            y_forward(NEAR, FAR, k, k, MINUS).wait_send()

        return 0

    lax.fori_loop(0, OWN, drain, 0)
    split_forward(MINUS).wait_send()
    split_forward(PLUS).wait_send()

    def drain_extra(slot, _):
        src = XNEAR.at[slot, 0, slab(c)]
        g = OWN + slot
        for d in (MINUS, PLUS):
            y_send(src, XNEAR, slot, g, d).wait_send()
        for kind in range(4):
            relay(src, XFAR if kind == 3 else XNEAR, slot, g, kind).wait_send()
        y_forward(XNEAR, XFAR, slot, g, MINUS).wait_send()
        return 0

    lax.fori_loop(0, extras, drain_extra, 0)

    def drain_col(d, _):
        col_copy(d).wait_send()
        return 0

    def drain_row(d, _):
        row_copy(d).wait_send()
        return 0

    lax.fori_loop(1, 8, drain_col, 0)
    lax.fori_loop(1, 16, drain_row, 0)


def per_device(inputs, out_grads, user_ids):
    dma = pltpu.SemaphoreType.DMA
    n = OWN + 2
    bf16, f32 = jnp.bfloat16, jnp.float32
    return pl.pallas_call(
        kernel,
        out_shape=jax.ShapeDtypeStruct((OWN * CH, BLOCK), bf16),
        in_specs=[
            pl.BlockSpec(memory_space=pltpu.SMEM),
            pl.BlockSpec(memory_space=pl.ANY),
            pl.BlockSpec(memory_space=pl.ANY),
        ],
        out_specs=pl.BlockSpec(memory_space=pltpu.VMEM),
        scratch_shapes=[
            pltpu.VMEM((OWN, 3, MB, CH), bf16),
            pltpu.VMEM((OWN, MB, CH), bf16),
            pltpu.VMEM((2, 3, MB, CH), bf16),
            pltpu.VMEM((2, MB, CH), bf16),
            pltpu.VMEM((2, 4, MB, HALF), bf16),
            pltpu.VMEM((n, 2, CH, BLOCK), bf16),
            pltpu.VMEM((BLOCK, BLOCK), bf16),
            pltpu.VMEM((BLOCK, BLOCK), bf16),
            pltpu.VMEM((BLOCK, BLOCK), bf16),
            pltpu.VMEM((CH, BLOCK), bf16),
            pltpu.VMEM((8, BLOCK), f32),
            pltpu.VMEM((8, 128), f32),
            pltpu.VMEM((8, 8, 128), f32),
            pltpu.VMEM((8, 128), f32),
            pltpu.VMEM((16, 8, 128), f32),
            dma((2, n)), dma((2, n)), dma((n,)), dma((n,)), dma((2,)), dma((2,)), dma((4, n)), dma((4, n)), dma((n,)), dma((3,)), dma((2,)),
            dma((2, 2)), dma((2, 2)), dma((2, 2)), dma((2, 2)),
            dma((2, 4, 2)), dma((2, 4, 2)), dma((2, 4, 2)), dma((2, 4, 2)), dma((2,)),
            dma((8,)), dma((8,)), dma((16,)), dma((16,)), dma, dma,
        ],
        compiler_params=pltpu.CompilerParams(
            collective_id=0, has_side_effects=True, vmem_limit_bytes=44 * 1024 * 1024
        ),
    )(user_ids, inputs, out_grads)


def solution(mesh):
    torus = Mesh(mesh.devices.reshape(4, 4, 4, 2), ("z", "x", "y", "c"))
    return jax.shard_map(
        per_device,
        mesh=torus,
        in_specs=(P(("y", "c"), ("z", "x")), P(("z", "x"), ("y", "c")), P()),
        out_specs=P(("z", "x"), ("y", "c")),
        check_vma=False,
    )
```

```python
import math

import jax
import jax.numpy as jnp
from jax import lax
from jax.experimental import pallas as pl
from jax.experimental.pallas import tpu as pltpu
from jax.sharding import Mesh
from jax.sharding import PartitionSpec as P

FF = 28672
D = 8192
BLOCK = 1024
MICRO = 4
TARGET = 0.15 * math.sqrt(FF * D / BLOCK)
LAST_SCALE = math.sqrt(BLOCK)

MESH = pl.DeviceIdType.MESH
CH = 256
OWN = 7
SLAB = 192
MB = 384
GS = 96
HALF = 512
MINUS, PLUS = 0, 1


def dot_tn(a, b):
    return lax.dot_general(a, b, (((0,), (0,)), ((), ())), preferred_element_type=jnp.float32)


def dot_nt(a, b):
    return lax.dot_general(a, b, (((1,), (1,)), ((), ())), preferred_element_type=jnp.float32)


def dot_nn(a, b):
    return lax.dot_general(a, b, (((1,), (0,)), ((), ())), preferred_element_type=jnp.float32)


def kernel(
    users, inp, og, out,
    uids, NEAR, FAR, XNEAR, XFAR, OG, G, X, X1, A, BACK, SQ, S1, R1, S2, R2,
    us, sy, ry, sf, rf, rh, sb0, rb0, sb3, rb3, lc, sx, rx, sxy, rxy, sxf, rxf, sxb, rxb,
    oa1s, oa1r, of1s, of1r, oa2s, oa2r, of2s, of2r, ol,
    a1s, a1r, a2s, a2r, ret_s, ret_r,
):
    z, x, y, c = (lax.axis_index(a) for a in ("z", "x", "y", "c"))
    zm, zp, zf = (lax.rem(z + d, 4) for d in (3, 1, 2))
    xm, xp, xf = (lax.rem(x + d, 4) for d in (3, 1, 2))
    ym, yp, yf = (lax.rem(y + d, 4) for d in (3, 1, 2))
    sib = 1 - c
    inner = jnp.logical_or(x == 1, x == 2)
    extras = jnp.where(inner, 2, 1)
    col = y * 2 + c
    row = z * 4 + x

    barrier = pltpu.get_barrier_semaphore()
    for dev in ((z, x, ym, c), (z, x, yp, c), (z, xm, y, c), (z, xp, y, c), (zm, x, y, c), (zp, x, y, c), (z, x, y, sib)):
        pl.semaphore_signal(barrier, inc=1, device_id=dev, device_id_type=MESH)
    pl.semaphore_wait(barrier, 7)

    def remote(src, dst, ss, rs, dev):
        return pltpu.make_async_remote_copy(
            src_ref=src, dst_ref=dst, send_sem=ss, recv_sem=rs, device_id=dev, device_id_type=MESH
        )

    ydev = [(z, x, ym, c), (z, x, yp, c)]
    xdev = [(z, xm, y, c), (z, xp, y, c)]
    zdev = [(zm, x, y, c), (zp, x, y, c)]
    sdev = (z, x, y, sib)

    def slab(cc):
        return pl.ds(pl.multiple_of(cc * SLAB, SLAB), SLAB)

    def extra(src_chunk, slot, direction, k):
        return remote(
            inp.at[:, pl.ds(src_chunk * CH, CH)], XNEAR.at[slot, 0, slab(c)], sx.at[k], rx.at[slot], xdev[direction]
        )

    def start_shared():
        @pl.when(x == 1)
        def _():
            extra(5, 0, PLUS, 0).start()
            extra(0, 0, MINUS, 1).start()
            extra(6, 1, PLUS, 2).start()

        @pl.when(x == 2)
        def _():
            extra(0, 0, MINUS, 0).start()
            extra(6, 0, PLUS, 1).start()
            extra(1, 1, MINUS, 2).start()

    users_copy = pltpu.make_async_copy(users, uids, us)
    users_copy.start()

    def grow(zz, xx):
        return zz, pl.ds(pl.multiple_of(xx * GS, GS), GS)

    def gpart(zz, xx, part):
        return zz, pl.ds(pl.multiple_of(xx * GS + part * (GS // 2), GS // 2), GS // 2)

    first_dev = [xdev, zdev]
    second_dev = [zdev, xdev]

    def along_first(h, d):
        if h == 0:
            return (z, [x, xm, xp, xf][d])
        return ([z, zm, zp, zf][d], x)

    def second_of(h, slot, d):
        zz, xx = along_first(h, slot)
        if h == 0:
            return ([z, zm, zp, zf][d], xx)
        return (zz, [x, xm, xp, xf][d])

    def first_send(h, direction):
        r = grow(z, x)
        return remote(
            og.at[:, pl.ds(h * HALF, HALF)], OG.at[h, r[0], r[1]], oa1s, oa1r.at[h, 1 - direction],
            first_dev[h][direction],
        )

    def first_wait(h, frm):
        r = grow(*along_first(h, 1 + frm))
        remote(OG.at[h, r[0], r[1]], OG.at[h, r[0], r[1]], oa1s, oa1r.at[h, frm], first_dev[h][frm]).wait_recv()

    def first_forward(h, frm):
        r = gpart(*along_first(h, 1 + frm), frm)
        return remote(
            OG.at[h, r[0], r[1]], OG.at[h, r[0], r[1]], of1s, of1r.at[h], first_dev[h][1 - frm]
        )

    def first_far_wait(h):
        r = grow(*along_first(h, 3))
        r = OG.at[h, r[0], r[1]]
        remote(r, r, of1s, of1r.at[h], first_dev[h][0]).wait_recv()

    def second_send(h, slot, direction):
        r = grow(*along_first(h, slot))
        src = og.at[:, pl.ds(h * HALF, HALF)] if slot == 0 else OG.at[h, r[0], r[1]]
        return remote(
            src, OG.at[h, r[0], r[1]], oa2s, oa2r.at[h, slot, 1 - direction], second_dev[h][direction]
        )

    def second_wait(h, slot, frm):
        r = grow(*second_of(h, slot, 1 + frm))
        remote(
            OG.at[h, r[0], r[1]], OG.at[h, r[0], r[1]], oa2s, oa2r.at[h, slot, frm], second_dev[h][frm]
        ).wait_recv()

    def second_forward(h, slot, frm):
        r = gpart(*second_of(h, slot, 1 + frm), frm)
        return remote(
            OG.at[h, r[0], r[1]], OG.at[h, r[0], r[1]], of2s, of2r, second_dev[h][1 - frm]
        )

    def second_far_wait():
        r = OG.at[0, 0:2]
        remote(r, r, of2s, of2r, xdev[0]).wait_recv()

    for h in (0, 1):
        for d in (MINUS, PLUS):
            first_send(h, d).start()
    for h in (0, 1):
        for d in (MINUS, PLUS):
            second_send(h, 0, d).start()

    place_of = (2, 1)

    def own_src(k):
        return inp.at[:, pl.ds(pl.multiple_of(k * CH, CH), CH)]

    def y_send(src, buf, k, ss, rs, direction):
        return remote(src, buf.at[k, place_of[1 - direction], slab(c)], ss, rs.at[1 - direction, k], ydev[direction])

    def y_wait(buf, k, rs, frm):
        r = buf.at[k, place_of[frm], slab(c)]
        remote(r, r, sf, rs.at[frm, k], ydev[frm]).wait_recv()

    def y_forward(buf, dst, k, ss, rs, frm):
        return remote(buf.at[k, place_of[frm], slab(c)], dst.at[k, slab(c)], ss, rs.at[k], ydev[1 - frm])

    def split_forward(frm):
        k = OWN - 1
        part = pl.ds(pl.multiple_of(c * SLAB + frm * (SLAB // 2), SLAB // 2), SLAB // 2)
        return remote(NEAR.at[k, place_of[frm], part], FAR.at[k, part], sf, rh.at[frm], ydev[1 - frm])

    def y_far_wait(dst, k, rs):
        r = dst.at[k, slab(c)]
        remote(r, r, sf, rs.at[k], ydev[0]).wait_recv()

    def relay(src, dst, k, ss, rs, kind):
        r = slab(c)
        return remote(src, dst.at[k, r] if kind == 3 else dst.at[k, (0, 2, 1)[kind], r], ss, rs, sdev)

    def relay_wait(dst, k, rs, kind):
        r = slab(sib)
        r = dst.at[k, r] if kind == 3 else dst.at[k, (0, 2, 1)[kind], r]
        remote(r, r, sf, rs, sdev).wait_recv()

    def local(k):
        return pltpu.make_async_copy(own_src(k), NEAR.at[k, 0, slab(c)], lc)

    def start_own(k, _):
        y_send(own_src(k), NEAR, k, sy, ry, MINUS).start()
        y_send(own_src(k), NEAR, k, sy, ry, PLUS).start()
        return 0

    lax.fori_loop(0, OWN, start_own, 0)

    def og_local(h):
        return pltpu.make_async_copy(og.at[:, pl.ds(h * HALF, HALF)], OG.at[(h, *grow(z, x))], ol.at[h])

    og_local(0).start()
    og_local(1).start()

    def start_near(k, _):
        local(k).start()
        relay(own_src(k), NEAR, k, sb0, rb0, 0).start()
        return 0

    lax.fori_loop(0, OWN, start_near, 0)

    for h in (1, 0):
        for frm in (MINUS, PLUS):
            first_wait(h, frm)
            first_forward(h, frm).start()
            for d in (MINUS, PLUS):
                second_send(h, 1 + frm, d).start()
    for h in (1, 0):
        for frm in (MINUS, PLUS):
            second_wait(h, 0, frm)
            second_forward(h, 0, frm).start()
    for h in (1, 0):
        first_far_wait(h)
        for d in (MINUS, PLUS):
            second_send(h, 3, d).start()
    for slot in (1, 2, 3):
        for h in (1, 0):
            for frm in (MINUS, PLUS):
                second_wait(h, slot, frm)
                second_forward(h, slot, frm).start()

    start_shared()

    def middle(k, _):
        for frm in (MINUS, PLUS):
            y_wait(NEAR, k, ry, frm)

            @pl.when(jnp.logical_and(lax.rem(k, 2) == frm, k < OWN - 1))
            def _():
                y_forward(NEAR, FAR, k, sf, rf, frm).start()

            relay(NEAR.at[k, place_of[frm], slab(c)], NEAR, k, sb0, rb0, 1 + frm).start()
        return 0

    lax.fori_loop(0, OWN, middle, 0)
    split_forward(MINUS).start()
    split_forward(PLUS).start()

    second_far_wait()
    og_local(0).wait()
    og_local(1).wait()

    own_slabs = NEAR.at[:, 0, slab(c)]
    pltpu.make_async_copy(own_slabs, own_slabs, lc).wait()
    sibling_slabs = NEAR.at[:, :, slab(sib)]
    remote(sibling_slabs, sibling_slabs, sb0, rb0, sdev).wait_recv()

    users_copy.wait()
    user_far = uids[yf]
    d1 = lax.rem(uids[yp] + user_far, 2)
    d2 = lax.rem(uids[ym] + user_far, 2)
    near_hit = (1 - d1) + 2 * d1 * (1 - d2)
    near_a = 1 - jnp.minimum(near_hit, 1)
    near_b = 2 - lax.div(near_hit, 2)

    def og_mb(place):
        return lax.rem(y + place + lax.div(place, 2), 4)

    mb_hit, mb_a, mb_b = og_mb(near_hit), og_mb(near_a), og_mb(near_b)
    SQ[...] = jnp.zeros_like(SQ)

    def grads(near, far, k, q, u, counted):
        for h in (0, 1):
            cols = slice(h * HALF, (h + 1) * HALF)
            if u == 1:
                rows_in = (near[k, near_a], near[k, near_b])
                rows_out = (OG[h, mb_a], OG[h, mb_b])
            else:
                rows_in = (near[k, near_hit], far[k])
                rows_out = (OG[h, mb_hit], OG[h, yf])
            p = dot_tn(jnp.concatenate(rows_in, axis=0), jnp.concatenate(rows_out, axis=0))
            G[q, u, :, cols] = p.astype(jnp.bfloat16)
            if counted:
                squares = p * p
                eight = squares[0:8]
                for e in range(1, CH // 8):
                    eight = eight + squares[8 * e : 8 * e + 8]
                SQ[u, :, cols] += eight

    def far_relay(k):
        if k == OWN - 1:
            for frm in (MINUS, PLUS):
                part = pl.ds(pl.multiple_of(c * SLAB + frm * (SLAB // 2), SLAB // 2), SLAB // 2)
                r = FAR.at[k, part]
                remote(r, r, sf, rh.at[frm], ydev[frm]).wait_recv()
        else:
            y_far_wait(FAR, k, rf)
        relay(FAR.at[k, slab(c)], FAR, k, sb3, rb3.at[k], 3).start()

    def start_extra(slot, _):
        src = XNEAR.at[slot, 0, slab(c)]
        remote(src, src, sx.at[0], rx.at[slot], xdev[0]).wait_recv()
        y_send(src, XNEAR, slot, sxy.at[MINUS, slot], rxy, MINUS).start()
        y_send(src, XNEAR, slot, sxy.at[PLUS, slot], rxy, PLUS).start()
        relay(src, XNEAR, slot, sxb.at[0, slot], rxb.at[0, slot], 0).start()
        return 0

    for k in range(OWN):
        grads(NEAR, FAR, k, k, 1, True)
        far_relay(k)
        if k == 2:
            lax.fori_loop(0, extras, start_extra, 0)
    for k in range(OWN):
        relay_wait(FAR, k, rb3.at[k], 3)
        grads(NEAR, FAR, k, k, 0, True)

    far_one = user_far.astype(jnp.float32)
    far_zero = 1.0 - far_one
    sums = []
    for u in (0, 1):
        lanes = SQ[u, :, 0:128]
        for j in range(1, 8):
            lanes = lanes + SQ[u, :, j * 128 : (j + 1) * 128]
        sums.append(jnp.sum(lanes, axis=0, keepdims=True))
    S2[...] = jnp.zeros_like(S2)
    S2[0:1] = sums[0] * far_zero + sums[1] * far_one
    S2[1:2] = sums[0] * far_one + sums[1] * far_zero

    def row_copy(d):
        p = lax.rem(row + d, 16)
        return remote(S2, R2.at[row], a2s, a2r, (lax.div(p, 4), lax.rem(p, 4), y, c))

    def row_start(d, _):
        row_copy(d).start()
        return 0

    lax.fori_loop(1, 16, row_start, 0)
    R2[row] = S2[...]

    def extra_middle(slot, _):
        for frm in (MINUS, PLUS):
            y_wait(XNEAR, slot, rxy, frm)

            @pl.when(slot == frm)
            def _():
                y_forward(XNEAR, XFAR, slot, sxf.at[slot], rxf, frm).start()

            relay(
                XNEAR.at[slot, place_of[frm], slab(c)], XNEAR, slot, sxb.at[1 + frm, slot], rxb.at[1 + frm, slot], 1 + frm
            ).start()
        return 0

    lax.fori_loop(0, extras, extra_middle, 0)
    others = R2.at[0:15]
    remote(others, others, a2s, a2r, sdev).wait_recv()
    total = R2[0]
    for j in range(1, 16):
        total = total + R2[j]
    S1[...] = total

    def col_copy(d):
        p = lax.rem(col + d, 8)
        return remote(S1, R1.at[col], a1s, a1r, (z, x, lax.div(p, 2), lax.rem(p, 2)))

    def col_start(d, _):
        col_copy(d).start()
        return 0

    lax.fori_loop(1, 8, col_start, 0)
    R1[col] = S1[...]

    def extra_far(slot, _):
        y_far_wait(XFAR, slot, rxf)
        relay(XFAR.at[slot, slab(c)], XFAR, slot, sxb.at[3, slot], rxb.at[3, slot], 3).start()
        return 0

    def extra_near_wait(slot, _):
        for kind in (0, 1, 2, 3):
            relay_wait(XFAR if kind == 3 else XNEAR, slot, rxb.at[kind, slot], kind)
        return 0

    lax.fori_loop(0, extras, extra_far, 0)
    lax.fori_loop(0, extras, extra_near_wait, 0)

    def extra_grads(slot, _):
        grads(XNEAR, XFAR, slot, OWN + slot, 1, False)
        grads(XNEAR, XFAR, slot, OWN + slot, 0, False)
        return 0

    lax.fori_loop(0, extras, extra_grads, 0)
    def sent(ref, sem):
        remote(ref, ref, sem, rb0, sdev).wait_send()

    sent(OG.at[0, 0], oa1s)
    sent(OG.at[0, 0, 0 : 2 * GS], of1s)
    sent(OG.at[0], oa2s)
    sent(OG.at[0, 0:2], of2s)
    sent(NEAR.at[:, 0:2, slab(c)], sy)
    sent(NEAR.at[:, :, slab(c)], sb0)
    sent(FAR.at[:, slab(c)], sf)
    sent(FAR.at[:, slab(c)], sb3)
    sent(R2.at[0:15], a2s)

    @pl.when(inner)
    def _():
        for k in range(3):
            sent(XNEAR.at[0, 0, slab(c)], sx.at[k])

    def drain_extra(slot, _):
        r = XNEAR.at[slot, 0, slab(c)]
        for d in (MINUS, PLUS):
            sent(r, sxy.at[d, slot])
        for kind in range(4):
            sent(r, sxb.at[kind, slot])
        sent(r, sxf.at[slot])
        return 0

    lax.fori_loop(0, extras, drain_extra, 0)
    others = R1.at[0:7]
    remote(others, others, a1s, a1r, sdev).wait_recv()
    total = R1[0]
    for j in range(1, 8):
        total = total + R1[j]
    factor = TARGET / jnp.sqrt(jnp.sum(total, axis=1, keepdims=True) + 1e-06)
    f_hit = factor[0:1, :] * far_zero + factor[1:2, :] * far_one
    f_other = factor[0:1, :] * far_one + factor[1:2, :] * far_zero

    right = x >= 2
    s1 = jnp.where(inner, 8, jnp.where(right, 0, 4))
    s2 = jnp.where(right, jnp.where(inner, 0, 1), 5)
    shared = [jnp.int32(7), s1, s2, s2 + 1]

    def give_back(direction):
        q = 0 if direction == PLUS else OWN - 1
        return remote(BACK, out.at[pl.ds(q * CH, CH)], ret_s, ret_r, xdev[direction])

    def chunk_of(t, i):
        return jnp.where(t == 0, shared[i], x + i)

    def gram_rows(src, i):
        r = slice(i * CH, (i + 1) * CH)
        t = dot_nt(src[r], src[i * CH :]).astype(jnp.bfloat16)
        A[r, i * CH :] = t
        for j in range(i + 1, 4):
            A[j * CH : (j + 1) * CH, r] = t[:, (j - i) * CH : (j - i + 1) * CH].T

    def finish(rows, gram):
        done = (1.5 * rows.astype(jnp.float32) - 0.5 * dot_nn(gram, X1[...])) * LAST_SCALE
        return done.astype(jnp.bfloat16)

    def put(t, i, value):
        out[pl.ds(pl.multiple_of(chunk_of(t, i) * CH, CH), CH)] = value

    def task(t, _):
        for i in range(4):
            q = chunk_of(t, i)
            X[i * CH : (i + 1) * CH] = (
                f_hit * G[q, 0].astype(jnp.float32) + f_other * G[q, 1].astype(jnp.float32)
            ).astype(jnp.bfloat16)
        for i in range(4):
            gram_rows(X, i)
        for i in range(4):
            r = slice(i * CH, (i + 1) * CH)
            X1[r] = (1.5 * X[r].astype(jnp.float32) - 0.5 * dot_nn(A[r], X[...])).astype(jnp.bfloat16)

        half = jnp.logical_and(t == 0, inner)

        @pl.when(half)
        def _():
            for i in (2, 3):
                r = slice(i * CH, (i + 1) * CH)
                put(t, i, finish(X1[r], dot_nt(X1[r], X1[...]).astype(jnp.bfloat16)))

        @pl.when(jnp.logical_not(half))
        def _():
            gram_rows(X1, 0)
            first = finish(X1[0:CH], A[0:CH])

            @pl.when(t == 0)
            def _():
                BACK[...] = first

                @pl.when(x == 0)
                def _():
                    give_back(PLUS).start()

                @pl.when(x == 3)
                def _():
                    give_back(MINUS).start()

            @pl.when(t == 1)
            def _():
                put(t, 0, first)

            for i in (1, 2, 3):
                gram_rows(X1, i)
            for i in (1, 2, 3):
                r = slice(i * CH, (i + 1) * CH)
                put(t, i, finish(X1[r], A[r]))

        return 0

    lax.fori_loop(0, 2, task, 0)
    sent(R1.at[0:7], a1s)

    @pl.when(x == 0)
    def _():
        give_back(PLUS).wait_send()

    @pl.when(x == 3)
    def _():
        give_back(MINUS).wait_send()

    @pl.when(x == 1)
    def _():
        give_back(PLUS).wait_recv()

    @pl.when(x == 2)
    def _():
        give_back(MINUS).wait_recv()


def per_device(inputs, out_grads, user_ids):
    dma = pltpu.SemaphoreType.DMA
    n = OWN + 2
    bf16, f32 = jnp.bfloat16, jnp.float32
    return pl.pallas_call(
        kernel,
        out_shape=jax.ShapeDtypeStruct((OWN * CH, BLOCK), bf16),
        in_specs=[pl.BlockSpec(memory_space=pltpu.HBM)] * 3,
        out_specs=pl.BlockSpec(memory_space=pltpu.VMEM),
        scratch_shapes=[
            pltpu.SMEM((MICRO,), jnp.int32),
            pltpu.VMEM((OWN, 3, MB, CH), bf16),
            pltpu.VMEM((OWN, MB, CH), bf16),
            pltpu.VMEM((2, 3, MB, CH), bf16),
            pltpu.VMEM((2, MB, CH), bf16),
            pltpu.VMEM((2, 4, MB, HALF), bf16),
            pltpu.VMEM((n, 2, CH, BLOCK), bf16),
            pltpu.VMEM((BLOCK, BLOCK), bf16),
            pltpu.VMEM((BLOCK, BLOCK), bf16),
            pltpu.VMEM((BLOCK, BLOCK), bf16),
            pltpu.VMEM((CH, BLOCK), bf16),
            pltpu.VMEM((2, 8, BLOCK), f32),
            pltpu.VMEM((8, 128), f32),
            pltpu.VMEM((8, 8, 128), f32),
            pltpu.VMEM((8, 128), f32),
            pltpu.VMEM((16, 8, 128), f32),
            dma, dma, dma((2, OWN)), dma, dma((OWN - 1,)), dma((2,)), dma, dma, dma, dma((OWN,)), dma,
            dma((3,)), dma((2,)), dma((2, 2)), dma((2, 2)), dma((2,)), dma((2,)), dma((4, 2)), dma((4, 2)),
            dma, dma((2, 2)), dma, dma((2,)), dma, dma((2, 4, 2)), dma, dma, dma((2,)),
            dma, dma, dma, dma, dma, dma,
        ],
        compiler_params=pltpu.CompilerParams(
            collective_id=0, has_side_effects=True, vmem_limit_bytes=44 * 1024 * 1024
        ),
    )(*(pltpu.with_memory_space_constraint(v, pltpu.HBM) for v in (user_ids, inputs, out_grads)))


def solution(mesh):
    torus = Mesh(mesh.devices.reshape(4, 4, 4, 2), ("z", "x", "y", "c"))
    return jax.shard_map(
        per_device,
        mesh=torus,
        in_specs=(P(("y", "c"), ("z", "x")), P(("z", "x"), ("y", "c")), P()),
        out_specs=P(("z", "x"), ("y", "c")),
        check_vma=False,
    )
```

```python
import math

import jax
import jax.numpy as jnp
from jax import lax
from jax.experimental import pallas as pl
from jax.experimental.pallas import tpu as pltpu
from jax.sharding import Mesh
from jax.sharding import PartitionSpec as P

FF = 28672
D = 8192
BLOCK = 1024
MICRO = 4
TARGET = 0.15 * math.sqrt(FF * D / BLOCK)
LAST_SCALE = math.sqrt(BLOCK)

MESH = pl.DeviceIdType.MESH
CH = 256
OWN = 7
SLAB = 192
MB = 384
GS = 96
HALF = 512
MINUS, PLUS = 0, 1


def dot_tn(a, b):
    return lax.dot_general(a, b, (((0,), (0,)), ((), ())), preferred_element_type=jnp.float32)


def dot_nt(a, b):
    return lax.dot_general(a, b, (((1,), (1,)), ((), ())), preferred_element_type=jnp.float32)


def dot_nn(a, b):
    return lax.dot_general(a, b, (((1,), (0,)), ((), ())), preferred_element_type=jnp.float32)


def kernel(
    users, inp, og, out,
    uids, NEAR, FAR, XNEAR, XFAR, OG, G, X, X1, A, BACK, SQ, S1, R1, S2, R2,
    us, sy, ry, sf, rf, rh, sb0, rb0, sb3, rb3, lc, sx, rx, sxy, rxy, sxf, rxf, sxb, rxb,
    oa1s, oa1r, of1s, of1r, oa2s, oa2r, of2s, of2r, ol,
    a1s, a1r, a2s, a2r, ret_s, ret_r,
):
    z, x, y, c = (lax.axis_index(a) for a in ("z", "x", "y", "c"))
    zm, zp, zf = (lax.rem(z + d, 4) for d in (3, 1, 2))
    xm, xp, xf = (lax.rem(x + d, 4) for d in (3, 1, 2))
    ym, yp, yf = (lax.rem(y + d, 4) for d in (3, 1, 2))
    sib = 1 - c
    inner = jnp.logical_or(x == 1, x == 2)
    extras = jnp.where(inner, 2, 1)
    col = y * 2 + c
    row = z * 4 + x

    barrier = pltpu.get_barrier_semaphore()
    for dev in ((z, x, ym, c), (z, x, yp, c), (z, xm, y, c), (z, xp, y, c), (zm, x, y, c), (zp, x, y, c), (z, x, y, sib)):
        pl.semaphore_signal(barrier, inc=1, device_id=dev, device_id_type=MESH)
    pl.semaphore_wait(barrier, 7)

    def remote(src, dst, ss, rs, dev):
        return pltpu.make_async_remote_copy(
            src_ref=src, dst_ref=dst, send_sem=ss, recv_sem=rs, device_id=dev, device_id_type=MESH
        )

    ydev = [(z, x, ym, c), (z, x, yp, c)]
    xdev = [(z, xm, y, c), (z, xp, y, c)]
    zdev = [(zm, x, y, c), (zp, x, y, c)]
    sdev = (z, x, y, sib)

    def slab(cc):
        return pl.ds(pl.multiple_of(cc * SLAB, SLAB), SLAB)

    def extra(src_chunk, slot, direction, k):
        return remote(
            inp.at[:, pl.ds(src_chunk * CH, CH)], XNEAR.at[slot, 0, slab(c)], sx.at[k], rx.at[slot], xdev[direction]
        )

    def start_shared():
        @pl.when(x == 1)
        def _():
            extra(5, 0, PLUS, 0).start()
            extra(0, 0, MINUS, 1).start()
            extra(6, 1, PLUS, 2).start()

        @pl.when(x == 2)
        def _():
            extra(0, 0, MINUS, 0).start()
            extra(6, 0, PLUS, 1).start()
            extra(1, 1, MINUS, 2).start()

    users_copy = pltpu.make_async_copy(users, uids, us)
    users_copy.start()

    def grow(zz, xx):
        return zz, pl.ds(pl.multiple_of(xx * GS, GS), GS)

    def gpart(zz, xx, part):
        return zz, pl.ds(pl.multiple_of(xx * GS + part * (GS // 2), GS // 2), GS // 2)

    first_dev = [xdev, zdev]
    second_dev = [zdev, xdev]

    def along_first(h, d):
        if h == 0:
            return (z, [x, xm, xp, xf][d])
        return ([z, zm, zp, zf][d], x)

    def second_of(h, slot, d):
        zz, xx = along_first(h, slot)
        if h == 0:
            return ([z, zm, zp, zf][d], xx)
        return (zz, [x, xm, xp, xf][d])

    def first_send(h, direction):
        r = grow(z, x)
        return remote(
            og.at[:, pl.ds(h * HALF, HALF)], OG.at[h, r[0], r[1]], oa1s, oa1r.at[h, 1 - direction],
            first_dev[h][direction],
        )

    def first_wait(h, frm):
        r = grow(*along_first(h, 1 + frm))
        remote(OG.at[h, r[0], r[1]], OG.at[h, r[0], r[1]], oa1s, oa1r.at[h, frm], first_dev[h][frm]).wait_recv()

    def first_forward(h, frm):
        r = gpart(*along_first(h, 1 + frm), frm)
        return remote(
            OG.at[h, r[0], r[1]], OG.at[h, r[0], r[1]], of1s, of1r.at[h], first_dev[h][1 - frm]
        )

    def first_far_wait(h):
        r = grow(*along_first(h, 3))
        r = OG.at[h, r[0], r[1]]
        remote(r, r, of1s, of1r.at[h], first_dev[h][0]).wait_recv()

    def second_send(h, slot, direction):
        r = grow(*along_first(h, slot))
        src = og.at[:, pl.ds(h * HALF, HALF)] if slot == 0 else OG.at[h, r[0], r[1]]
        return remote(
            src, OG.at[h, r[0], r[1]], oa2s, oa2r.at[h, slot, 1 - direction], second_dev[h][direction]
        )

    def second_wait(h, slot, frm):
        r = grow(*second_of(h, slot, 1 + frm))
        remote(
            OG.at[h, r[0], r[1]], OG.at[h, r[0], r[1]], oa2s, oa2r.at[h, slot, frm], second_dev[h][frm]
        ).wait_recv()

    def second_forward(h, slot, frm):
        r = gpart(*second_of(h, slot, 1 + frm), frm)
        return remote(
            OG.at[h, r[0], r[1]], OG.at[h, r[0], r[1]], of2s, of2r, second_dev[h][1 - frm]
        )

    def second_far_wait():
        r = OG.at[0, 0:2]
        remote(r, r, of2s, of2r, xdev[0]).wait_recv()

    for h in (0, 1):
        for d in (MINUS, PLUS):
            first_send(h, d).start()
    for h in (0, 1):
        for d in (MINUS, PLUS):
            second_send(h, 0, d).start()

    place_of = (2, 1)

    def own_src(k):
        return inp.at[:, pl.ds(pl.multiple_of(k * CH, CH), CH)]

    def y_send(src, buf, k, ss, rs, direction):
        return remote(src, buf.at[k, place_of[1 - direction], slab(c)], ss, rs.at[1 - direction, k], ydev[direction])

    def y_wait(buf, k, rs, frm):
        r = buf.at[k, place_of[frm], slab(c)]
        remote(r, r, sf, rs.at[frm, k], ydev[frm]).wait_recv()

    def y_forward(buf, dst, k, ss, rs, frm):
        return remote(buf.at[k, place_of[frm], slab(c)], dst.at[k, slab(c)], ss, rs.at[k], ydev[1 - frm])

    def split_forward(frm):
        k = OWN - 1
        part = pl.ds(pl.multiple_of(c * SLAB + frm * (SLAB // 2), SLAB // 2), SLAB // 2)
        return remote(NEAR.at[k, place_of[frm], part], FAR.at[k, part], sf, rh.at[frm], ydev[1 - frm])

    def y_far_wait(dst, k, rs):
        r = dst.at[k, slab(c)]
        remote(r, r, sf, rs.at[k], ydev[0]).wait_recv()

    def relay(src, dst, k, ss, rs, kind):
        r = slab(c)
        return remote(src, dst.at[k, r] if kind == 3 else dst.at[k, (0, 2, 1)[kind], r], ss, rs, sdev)

    def relay_wait(dst, k, rs, kind):
        r = slab(sib)
        r = dst.at[k, r] if kind == 3 else dst.at[k, (0, 2, 1)[kind], r]
        remote(r, r, sf, rs, sdev).wait_recv()

    def local(k):
        return pltpu.make_async_copy(own_src(k), NEAR.at[k, 0, slab(c)], lc)

    def start_own(k, _):
        y_send(own_src(k), NEAR, k, sy, ry, MINUS).start()
        y_send(own_src(k), NEAR, k, sy, ry, PLUS).start()
        return 0

    lax.fori_loop(0, OWN, start_own, 0)

    def og_local(h):
        return pltpu.make_async_copy(og.at[:, pl.ds(h * HALF, HALF)], OG.at[(h, *grow(z, x))], ol.at[h])

    og_local(0).start()
    og_local(1).start()

    def start_near(k, _):
        local(k).start()
        relay(own_src(k), NEAR, k, sb0, rb0, 0).start()
        return 0

    lax.fori_loop(0, OWN, start_near, 0)

    for h in (1, 0):
        for frm in (MINUS, PLUS):
            first_wait(h, frm)
            first_forward(h, frm).start()
            for d in (MINUS, PLUS):
                second_send(h, 1 + frm, d).start()
    for h in (1, 0):
        for frm in (MINUS, PLUS):
            second_wait(h, 0, frm)
            second_forward(h, 0, frm).start()
    for h in (1, 0):
        first_far_wait(h)
        for d in (MINUS, PLUS):
            second_send(h, 3, d).start()
    for slot in (1, 2, 3):
        for h in (1, 0):
            for frm in (MINUS, PLUS):
                second_wait(h, slot, frm)
                second_forward(h, slot, frm).start()

    start_shared()

    def middle(k, _):
        for frm in (MINUS, PLUS):
            y_wait(NEAR, k, ry, frm)

            @pl.when(jnp.logical_and(lax.rem(k, 2) == frm, k < OWN - 1))
            def _():
                y_forward(NEAR, FAR, k, sf, rf, frm).start()

            relay(NEAR.at[k, place_of[frm], slab(c)], NEAR, k, sb0, rb0, 1 + frm).start()
        return 0

    lax.fori_loop(0, OWN, middle, 0)
    split_forward(MINUS).start()
    split_forward(PLUS).start()

    second_far_wait()
    og_local(0).wait()
    og_local(1).wait()

    own_slabs = NEAR.at[:, 0, slab(c)]
    pltpu.make_async_copy(own_slabs, own_slabs, lc).wait()
    sibling_slabs = NEAR.at[:, :, slab(sib)]
    remote(sibling_slabs, sibling_slabs, sb0, rb0, sdev).wait_recv()

    users_copy.wait()
    user_far = uids[yf]
    d1 = lax.rem(uids[yp] + user_far, 2)
    d2 = lax.rem(uids[ym] + user_far, 2)
    near_hit = (1 - d1) + 2 * d1 * (1 - d2)
    near_a = 1 - jnp.minimum(near_hit, 1)
    near_b = 2 - lax.div(near_hit, 2)

    def og_mb(place):
        return lax.rem(y + place + lax.div(place, 2), 4)

    mb_hit, mb_a, mb_b = og_mb(near_hit), og_mb(near_a), og_mb(near_b)
    SQ[...] = jnp.zeros_like(SQ)

    def grads(near, far, k, q, u, counted):
        for h in (0, 1):
            cols = slice(h * HALF, (h + 1) * HALF)
            if u == 1:
                rows_in = (near[k, near_a], near[k, near_b])
                rows_out = (OG[h, mb_a], OG[h, mb_b])
            else:
                rows_in = (near[k, near_hit], far[k])
                rows_out = (OG[h, mb_hit], OG[h, yf])
            p = dot_tn(jnp.concatenate(rows_in, axis=0), jnp.concatenate(rows_out, axis=0))
            G[q, u, :, cols] = p.astype(jnp.bfloat16)
            if counted:
                squares = p * p
                eight = squares[0:8]
                for e in range(1, CH // 8):
                    eight = eight + squares[8 * e : 8 * e + 8]
                SQ[u, :, cols] += eight

    def far_relay(k):
        if k == OWN - 1:
            for frm in (MINUS, PLUS):
                part = pl.ds(pl.multiple_of(c * SLAB + frm * (SLAB // 2), SLAB // 2), SLAB // 2)
                r = FAR.at[k, part]
                remote(r, r, sf, rh.at[frm], ydev[frm]).wait_recv()
        else:
            y_far_wait(FAR, k, rf)
        relay(FAR.at[k, slab(c)], FAR, k, sb3, rb3.at[k], 3).start()

    def start_extra(slot, _):
        src = XNEAR.at[slot, 0, slab(c)]
        remote(src, src, sx.at[0], rx.at[slot], xdev[0]).wait_recv()
        y_send(src, XNEAR, slot, sxy.at[MINUS, slot], rxy, MINUS).start()
        y_send(src, XNEAR, slot, sxy.at[PLUS, slot], rxy, PLUS).start()
        relay(src, XNEAR, slot, sxb.at[0, slot], rxb.at[0, slot], 0).start()
        return 0

    for k in range(OWN):
        grads(NEAR, FAR, k, k, 1, True)
        far_relay(k)
        if k == 4:
            lax.fori_loop(0, extras, start_extra, 0)
    for k in range(OWN):
        relay_wait(FAR, k, rb3.at[k], 3)
        grads(NEAR, FAR, k, k, 0, True)

    far_one = user_far.astype(jnp.float32)
    far_zero = 1.0 - far_one
    sums = []
    for u in (0, 1):
        lanes = SQ[u, :, 0:128]
        for j in range(1, 8):
            lanes = lanes + SQ[u, :, j * 128 : (j + 1) * 128]
        sums.append(jnp.sum(lanes, axis=0, keepdims=True))
    S2[...] = jnp.zeros_like(S2)
    S2[0:1] = sums[0] * far_zero + sums[1] * far_one
    S2[1:2] = sums[0] * far_one + sums[1] * far_zero

    def row_copy(d):
        p = lax.rem(row + d, 16)
        return remote(S2, R2.at[row], a2s, a2r, (lax.div(p, 4), lax.rem(p, 4), y, c))

    def row_start(d, _):
        row_copy(d).start()
        return 0

    lax.fori_loop(1, 16, row_start, 0)
    R2[row] = S2[...]

    def extra_middle(slot, _):
        for frm in (MINUS, PLUS):
            y_wait(XNEAR, slot, rxy, frm)

            @pl.when(slot == frm)
            def _():
                y_forward(XNEAR, XFAR, slot, sxf.at[slot], rxf, frm).start()

            relay(
                XNEAR.at[slot, place_of[frm], slab(c)], XNEAR, slot, sxb.at[1 + frm, slot], rxb.at[1 + frm, slot], 1 + frm
            ).start()
        return 0

    lax.fori_loop(0, 1, extra_middle, 0)
    others = R2.at[0:15]
    remote(others, others, a2s, a2r, sdev).wait_recv()
    total = R2[0]
    for j in range(1, 16):
        total = total + R2[j]
    S1[...] = total

    def col_copy(d):
        p = lax.rem(col + d, 8)
        return remote(S1, R1.at[col], a1s, a1r, (z, x, lax.div(p, 2), lax.rem(p, 2)))

    def col_start(d, _):
        col_copy(d).start()
        return 0

    lax.fori_loop(1, 8, col_start, 0)
    R1[col] = S1[...]

    def extra_far(slot, _):
        y_far_wait(XFAR, slot, rxf)
        relay(XFAR.at[slot, slab(c)], XFAR, slot, sxb.at[3, slot], rxb.at[3, slot], 3).start()
        return 0

    def extra_near_wait(slot, _):
        for kind in (0, 1, 2):
            relay_wait(XNEAR, slot, rxb.at[kind, slot], kind)
        return 0

    lax.fori_loop(1, extras, extra_middle, 0)
    lax.fori_loop(0, extras, extra_near_wait, 0)

    def extra_other(slot, _):
        grads(XNEAR, XFAR, slot, OWN + slot, 1, False)
        return 0

    def extra_hit(slot, _):
        relay_wait(XFAR, slot, rxb.at[3, slot], 3)
        grads(XNEAR, XFAR, slot, OWN + slot, 0, False)
        return 0

    lax.fori_loop(0, extras, extra_other, 0)
    lax.fori_loop(0, extras, extra_far, 0)
    lax.fori_loop(0, extras, extra_hit, 0)
    def sent(ref, sem):
        remote(ref, ref, sem, rb0, sdev).wait_send()

    sent(OG.at[0, 0], oa1s)
    sent(OG.at[0, 0, 0 : 2 * GS], of1s)
    sent(OG.at[0], oa2s)
    sent(OG.at[0, 0:2], of2s)
    sent(NEAR.at[:, 0:2, slab(c)], sy)
    sent(NEAR.at[:, :, slab(c)], sb0)
    sent(FAR.at[:, slab(c)], sf)
    sent(FAR.at[:, slab(c)], sb3)
    sent(R2.at[0:15], a2s)

    @pl.when(inner)
    def _():
        for k in range(3):
            sent(XNEAR.at[0, 0, slab(c)], sx.at[k])

    def drain_extra(slot, _):
        r = XNEAR.at[slot, 0, slab(c)]
        for d in (MINUS, PLUS):
            sent(r, sxy.at[d, slot])
        for kind in range(4):
            sent(r, sxb.at[kind, slot])
        sent(r, sxf.at[slot])
        return 0

    lax.fori_loop(0, extras, drain_extra, 0)
    others = R1.at[0:7]
    remote(others, others, a1s, a1r, sdev).wait_recv()
    total = R1[0]
    for j in range(1, 8):
        total = total + R1[j]
    factor = TARGET / jnp.sqrt(jnp.sum(total, axis=1, keepdims=True) + 1e-06)
    f_hit = factor[0:1, :] * far_zero + factor[1:2, :] * far_one
    f_other = factor[0:1, :] * far_one + factor[1:2, :] * far_zero

    right = x >= 2
    s1 = jnp.where(inner, 8, jnp.where(right, 0, 4))
    s2 = jnp.where(right, jnp.where(inner, 0, 1), 5)
    shared = [jnp.int32(7), s1, s2, s2 + 1]

    def give_back(direction, part):
        q = 0 if direction == PLUS else OWN - 1
        return remote(
            BACK.at[pl.ds(part * CH // 2, CH // 2)], out.at[pl.ds(q * CH + part * CH // 2, CH // 2)],
            ret_s.at[part], ret_r.at[part], xdev[direction],
        )

    def chunk_of(t, i):
        return jnp.where(t == 0, shared[i], x + i)

    def gram_rows(src, i):
        r = slice(i * CH, (i + 1) * CH)
        t = dot_nt(src[r], src[i * CH :]).astype(jnp.bfloat16)
        A[r, i * CH :] = t
        for j in range(i + 1, 4):
            A[j * CH : (j + 1) * CH, r] = t[:, (j - i) * CH : (j - i + 1) * CH].T

    def finish(rows, gram):
        done = (1.5 * rows.astype(jnp.float32) - 0.5 * dot_nn(gram, X1[...])) * LAST_SCALE
        return done.astype(jnp.bfloat16)

    def put(t, i, value):
        out[pl.ds(pl.multiple_of(chunk_of(t, i) * CH, CH), CH)] = value

    def task(t, _):
        for i in range(4):
            q = chunk_of(t, i)
            X[i * CH : (i + 1) * CH] = (
                f_hit * G[q, 0].astype(jnp.float32) + f_other * G[q, 1].astype(jnp.float32)
            ).astype(jnp.bfloat16)
        for i in range(4):
            gram_rows(X, i)
        for i in range(4):
            r = slice(i * CH, (i + 1) * CH)
            X1[r] = (1.5 * X[r].astype(jnp.float32) - 0.5 * dot_nn(A[r], X[...])).astype(jnp.bfloat16)

        half = jnp.logical_and(t == 0, inner)

        @pl.when(half)
        def _():
            for i in (2, 3):
                r = slice(i * CH, (i + 1) * CH)
                put(t, i, finish(X1[r], dot_nt(X1[r], X1[...]).astype(jnp.bfloat16)))

        @pl.when(jnp.logical_not(half))
        def _():
            gram_rows(X1, 0)

            @pl.when(t == 0)
            def _():
                for part in (0, 1):
                    r = slice(part * CH // 2, (part + 1) * CH // 2)
                    BACK[r] = finish(X1[r], A[r])

                    @pl.when(x == 0)
                    def _():
                        give_back(PLUS, part).start()

                    @pl.when(x == 3)
                    def _():
                        give_back(MINUS, part).start()

            @pl.when(t == 1)
            def _():
                put(t, 0, finish(X1[0:CH], A[0:CH]))

            for i in (1, 2, 3):
                gram_rows(X1, i)
            for i in (1, 2, 3):
                r = slice(i * CH, (i + 1) * CH)
                put(t, i, finish(X1[r], A[r]))

        return 0

    lax.fori_loop(0, 2, task, 0)
    sent(R1.at[0:7], a1s)

    @pl.when(x == 0)
    def _():
        for part in (0, 1):
            give_back(PLUS, part).wait_send()

    @pl.when(x == 3)
    def _():
        for part in (0, 1):
            give_back(MINUS, part).wait_send()

    @pl.when(x == 1)
    def _():
        for part in (0, 1):
            give_back(PLUS, part).wait_recv()

    @pl.when(x == 2)
    def _():
        for part in (0, 1):
            give_back(MINUS, part).wait_recv()


def per_device(inputs, out_grads, user_ids):
    dma = pltpu.SemaphoreType.DMA
    n = OWN + 2
    bf16, f32 = jnp.bfloat16, jnp.float32
    return pl.pallas_call(
        kernel,
        out_shape=jax.ShapeDtypeStruct((OWN * CH, BLOCK), bf16),
        in_specs=[pl.BlockSpec(memory_space=pltpu.HBM)] * 3,
        out_specs=pl.BlockSpec(memory_space=pltpu.VMEM),
        scratch_shapes=[
            pltpu.SMEM((MICRO,), jnp.int32),
            pltpu.VMEM((OWN, 3, MB, CH), bf16),
            pltpu.VMEM((OWN, MB, CH), bf16),
            pltpu.VMEM((2, 3, MB, CH), bf16),
            pltpu.VMEM((2, MB, CH), bf16),
            pltpu.VMEM((2, 4, MB, HALF), bf16),
            pltpu.VMEM((n, 2, CH, BLOCK), bf16),
            pltpu.VMEM((BLOCK, BLOCK), bf16),
            pltpu.VMEM((BLOCK, BLOCK), bf16),
            pltpu.VMEM((BLOCK, BLOCK), bf16),
            pltpu.VMEM((CH, BLOCK), bf16),
            pltpu.VMEM((2, 8, BLOCK), f32),
            pltpu.VMEM((8, 128), f32),
            pltpu.VMEM((8, 8, 128), f32),
            pltpu.VMEM((8, 128), f32),
            pltpu.VMEM((16, 8, 128), f32),
            dma, dma, dma((2, OWN)), dma, dma((OWN - 1,)), dma((2,)), dma, dma, dma, dma((OWN,)), dma,
            dma((3,)), dma((2,)), dma((2, 2)), dma((2, 2)), dma((2,)), dma((2,)), dma((4, 2)), dma((4, 2)),
            dma, dma((2, 2)), dma, dma((2,)), dma, dma((2, 4, 2)), dma, dma, dma((2,)),
            dma, dma, dma, dma, dma((2,)), dma((2,)),
        ],
        compiler_params=pltpu.CompilerParams(
            collective_id=0, has_side_effects=True, vmem_limit_bytes=44 * 1024 * 1024
        ),
    )(*(pltpu.with_memory_space_constraint(v, pltpu.HBM) for v in (user_ids, inputs, out_grads)))


def solution(mesh):
    torus = Mesh(mesh.devices.reshape(4, 4, 4, 2), ("z", "x", "y", "c"))
    return jax.shard_map(
        per_device,
        mesh=torus,
        in_specs=(P(("y", "c"), ("z", "x")), P(("z", "x"), ("y", "c")), P()),
        out_specs=P(("z", "x"), ("y", "c")),
        check_vma=False,
    )
```
